32 devices in a mesh: ctx: 4 (over y, x), tp: 4 (over z), grp: 2 (over core).
Axes of the slice: x: 2, y: 2, z: 4, core: 2. Of those that a mesh axis runs over, the one named last changes fastest.
Arguments:
- patches: bfloat16 [32, 5120], P('ctx'), may hold values from -6 to 6
- route_count: int32 [4, 4], replicated, may hold values from 0 to 2, as said below
- text_states: bfloat16 [512, 4096], P('ctx', ('tp', 'grp')), may hold values from -6 to 6
- segment_ids: int32 [512], replicated, may hold values from 0 to 3, never falling along the last dimension, each value on 1 to 256 neighbouring positions
- vision_gain: float32 [1280], replicated, may hold values from 0.1 to 1.9
- merge_up: bfloat16 [5120, 2560], P(None, ('tp', 'grp')), may hold values from -0.078125 to 0.078125
- merge_down: bfloat16 [2560, 4096], P(('tp', 'grp')), may hold values from -0.125 to 0.125
- norm_gain: float32 [4096], replicated, may hold values from 0.1 to 1.9
- query_weight: bfloat16 [4096, 4096], P(None, ('tp', 'grp')), may hold values from -0.62928387 to 0.62928387
- kv_weight: bfloat16 [4096, 2048], P(None, 'tp'), may hold values from -0.4578688 to 0.4578688
Outputs:
- attended: bfloat16 [512, 4096], P('ctx', ('tp', 'grp'))
The draws below stay inside these ranges and needn't reach their ends.
Inputs may be any that keep to these rules, and one draw needn't show every extreme that they name: route_count[c, d] counts the live rows among the 2 rows that source c holds for owner d; at least one owner gets 2 live rows from every source. `segment_ids`: never falling along the packed batch; a segment has at most 256 positions.
All inputs are finite; a program needn't handle non-finite values.
Results may differ from the reference program's by a relative error of at most 0.04.
Values may be sent and summed in bfloat16 or wider, within the bound.
A program may use at most 64 MiB of HBM per device.

```python
import math
import jax
import jax.numpy as jnp
import numpy as np
from jax import lax

VIS = 1280
DIN = 5120
F = 2560
D = 4096
HQ = 32
KVH = 8
HD = 128
CAP = 2
TOK_DEV = 128
TOKENS = 512
PATCH_ROWS = 32
N_CTX = 4


def draw_route_count(key, part):
    counts_low = jax.random.randint(jax.random.fold_in(key, 11), (N_CTX, N_CTX), 0, CAP + 1)
    full_owner = jax.random.randint(jax.random.fold_in(key, 12), (), 0, N_CTX)
    full_column = jnp.arange(N_CTX)[None, :] == full_owner
    return jnp.where(full_column, CAP, counts_low).astype(jnp.int32)


def draw_query_weight(key, part):
    base = jnp.clip(jax.random.normal(jax.random.fold_in(key, 911), (D, HQ * HD), jnp.float32), -6.0, 6.0) * (8.0 / D) ** 0.5
    return base.astype(jnp.bfloat16)


def draw_kv_weight(key, part):
    base = jnp.clip(jax.random.normal(jax.random.fold_in(key, 921), (D, 2 * KVH * HD), jnp.float32), -6.0, 6.0) * D ** (-0.5)
    return base.astype(jnp.bfloat16)


def block_scale(own_key, dims, shards, smallest, top_value):
    def one(axis_at, blocks):
        draws = jax.random.uniform(jax.random.fold_in(jax.random.fold_in(own_key, 6), axis_at), (blocks,), jnp.float32, smallest / len(shards), top_value / len(shards))
        return jnp.repeat(jnp.exp(draws), dims[axis_at] // blocks).reshape((-1,) + (1,) * (len(dims) - axis_at - 1))

    loudness = one(*shards[0])
    for cut in shards[1:]:
        loudness = loudness * one(*cut)
    return loudness


def split_up(amount, total, reach, skew):
    loads = [(1 << 20) // math.isqrt(rank ** skew) + 1 for rank in range(2, amount + 1)]
    rest, counts = total - reach - (amount - 1), [1] * (amount - 1)
    while rest > 0:
        free = [i for i in range(amount - 1) if counts[i] < reach]
        whole, remaining = sum([loads[i] for i in free]), rest
        for i in free:
            extra = min(reach - counts[i], max(1, remaining * loads[i] // whole), rest)
            counts[i] = counts[i] + extra
            rest = rest - extra
    return np.array([reach] + counts)


def ragged(stream_key, count, total, most, slope):
    if count == 2:
        one = jax.random.randint(stream_key, (), max(1, total - most), min(most, total - 1) + 1)
        return jnp.stack([one, total - one])
    sizes = jnp.asarray(split_up(count, total, most, slope), jnp.int32)
    pairs = (count - 1) // 2
    source_of, receiver = sizes[1:1 + 2 * pairs:2], sizes[2:2 + 2 * pairs:2]
    room = jnp.minimum(source_of - 1, most - receiver)
    passed = jax.random.randint(jax.random.fold_in(stream_key, 1), (pairs,), 0, 1 << 20) % (room + 1)
    sizes = sizes.at[1:1 + 2 * pairs:2].set(source_of - passed).at[2:2 + 2 * pairs:2].set(receiver + passed)
    return sizes[jax.random.permutation(jax.random.fold_in(stream_key, 2), count)]


def noise(own_key, shape, scale, limit, shards=(), held_as=jnp.bfloat16):
    drawn = scale * jax.random.normal(own_key, shape, jnp.float32)
    if shards:
        drawn = drawn * block_scale(own_key, shape, shards, -0.22, 0.18)
    return jnp.clip(drawn, -limit, limit).astype(held_as)


def setup_inputs(seed: int = 0) -> dict:
    seeds = jax.random.split(jax.random.key(seed), 11)
    return {
        "patches": noise(seeds[0], (PATCH_ROWS, DIN), 1.0, 6.0, ((0, 4),)),
        "route_count": draw_route_count(jax.random.fold_in(seeds[10], 71), 0),
        "text_states": noise(seeds[2], (TOKENS, D), 1.0, 6.0, ((0, 4), (1, 8))),
        "segment_ids": jnp.searchsorted(jnp.cumsum(ragged(seeds[3], 4, TOKENS, TOKENS // 2, 0)), jnp.arange(TOKENS), side="right").astype(jnp.int32),
        "vision_gain": jnp.clip(1.0 + 0.18 * jax.random.normal(seeds[4], (VIS,), jnp.float32), 0.1, 1.9),
        "merge_up": noise(seeds[5], (DIN, F), DIN ** -0.5, 0.078125, ((1, 8),)),
        "merge_down": noise(seeds[6], (F, D), F ** -0.5, 0.125, ((0, 8),)),
        "norm_gain": jnp.clip(1.0 + 0.18 * jax.random.normal(seeds[7], (D,), jnp.float32), 0.1, 1.9),
        "query_weight": draw_query_weight(jax.random.fold_in(seeds[10], 71), 0),
        "kv_weight": draw_kv_weight(jax.random.fold_in(seeds[10], 71), 0),
    }


EPSILON = 1e-06
NEGATIVE = -1e+30

def reference(patches, route_count, text_states, segment_ids, vision_gain, merge_up, merge_down, norm_gain, query_weight, kv_weight):
    grouped = patches.astype(jnp.float32).reshape(PATCH_ROWS, 4, VIS)
    mean_square = lax.optimization_barrier(jnp.mean(grouped * grouped, axis=-1, keepdims=True))
    patch_normed = (grouped * lax.rsqrt(mean_square + EPSILON) * vision_gain).reshape(PATCH_ROWS, DIN).astype(jnp.bfloat16)
    hidden = jax.nn.gelu(jnp.dot(patch_normed, merge_up, preferred_element_type=jnp.float32), approximate=False).astype(jnp.bfloat16)
    merged = jnp.dot(hidden, merge_down, preferred_element_type=jnp.float32).astype(jnp.bfloat16)
    by_owner = merged.reshape(N_CTX, N_CTX, CAP, D).transpose(1, 0, 2, 3).reshape(N_CTX, N_CTX * CAP, D)
    count_ends = jnp.cumsum(route_count, axis=0).astype(jnp.int32)
    count_starts = (count_ends - route_count).astype(jnp.int32)
    slot_ids = jnp.arange(TOK_DEV, dtype=jnp.int32)
    source = lax.optimization_barrier(jnp.sum((count_ends.T[:, None, :] <= slot_ids[None, :, None]).astype(jnp.int32), axis=2)).astype(jnp.int32)
    source = jnp.minimum(source, N_CTX - 1)
    source_match = source[:, :, None] == jnp.arange(N_CTX, dtype=jnp.int32)[None, None, :]
    first_slot = lax.optimization_barrier(jnp.sum(jnp.where(source_match, count_starts.T[:, None, :], 0), axis=2)).astype(jnp.int32)
    visual = slot_ids[None, :] < count_ends[N_CTX - 1][:, None]
    pick_rows = jnp.where(visual, source * CAP + slot_ids[None, :] - first_slot, 0).astype(jnp.int32)
    visual_rows = jnp.take_along_axis(by_owner, pick_rows[:, :, None], axis=1)
    packed = jnp.where(visual[:, :, None], visual_rows, text_states.reshape(N_CTX, TOK_DEV, D)).reshape(TOKENS, D)
    packed_f = packed.astype(jnp.float32)
    mean_packed = lax.optimization_barrier(jnp.mean(packed_f * packed_f, axis=-1, keepdims=True))
    normal = (packed_f * lax.rsqrt(mean_packed + EPSILON) * norm_gain).astype(jnp.bfloat16)
    queries = jnp.dot(normal, query_weight, preferred_element_type=jnp.float32).astype(jnp.bfloat16).reshape(TOKENS, HQ, HD)
    kv_pairs = jnp.dot(normal, kv_weight, preferred_element_type=jnp.float32).astype(jnp.bfloat16).reshape(TOKENS, KVH, 2, HD)
    positions = jnp.arange(TOKENS, dtype=jnp.int32)
    visual_count = lax.optimization_barrier(jnp.sum(route_count, axis=0)).astype(jnp.int32)
    key_visual = positions % TOK_DEV < jnp.repeat(visual_count, TOK_DEV)
    allowed = (segment_ids[:, None] == segment_ids[None, :]) & (key_visual[None, :] | (positions[None, :] <= positions[:, None]))
    group = HQ // KVH

    def one_head(head_index):
        query_head = lax.dynamic_index_in_dim(queries, head_index, 1, keepdims=False)
        kv_pair = lax.dynamic_index_in_dim(kv_pairs, head_index // group, 1, keepdims=False)
        key_head = kv_pair[:, 0]
        value_head = kv_pair[:, 1]
        scores = jnp.dot(query_head, key_head.T, preferred_element_type=jnp.float32) * HD ** (-0.5)
        masked = jnp.where(allowed, scores, NEGATIVE)
        row_max = lax.optimization_barrier(jnp.max(masked, axis=1, keepdims=True))
        weights = jnp.where(allowed, jnp.exp(masked - row_max), 0.0)
        denominator = lax.optimization_barrier(jnp.sum(weights, axis=1, keepdims=True))
        mixed = jnp.dot(weights.astype(jnp.bfloat16), value_head, preferred_element_type=jnp.float32)
        return (mixed / denominator).astype(jnp.bfloat16)
    heads = lax.map(one_head, jnp.arange(HQ, dtype=jnp.int32))
    return heads.transpose(1, 0, 2).reshape(TOKENS, HQ * HD)
```

```python
import functools

import jax
import jax.numpy as jnp
from jax import lax
from jax.experimental import pallas as pl
from jax.experimental.pallas import tpu as pltpu
from jax.sharding import PartitionSpec as P

HQ = 32
KVH = 8
HD = 128


EPSILON = 1e-06
NEGATIVE = -1e30


def rms_scale(values, gain):
    mean_square = jnp.mean(values * values, axis=-1, keepdims=True)
    return values * lax.rsqrt(mean_square + EPSILON) * gain


def attend(
    running,
    queries4,
    shard_piece,
    key_pos,
    query_pos,
    query_seg,
    segment_ids,
    visual_count,
    tokens_dev,
):
    weighted, running_max, denominator = running
    piece_rows = shard_piece.shape[0]
    kv_heads = queries4.shape[1]
    kv_split = shard_piece.reshape(piece_rows, kv_heads, 2, HD)
    key_block = kv_split[:, :, 0]
    value_block = kv_split[:, :, 1]
    key_owner = key_pos // tokens_dev
    owner_match = key_owner[:, None] == jnp.arange(visual_count.shape[0], dtype=jnp.int32)[None, :]
    visual_limit = jnp.sum(jnp.where(owner_match, visual_count[None, :], 0), axis=1)
    key_visual = key_pos % tokens_dev < visual_limit
    key_seg = segment_ids[key_pos]
    allowed = (query_seg[:, None] == key_seg[None, :]) & (
        key_visual[None, :] | (key_pos[None, :] <= query_pos[:, None])
    )
    scores = jnp.where(
        allowed,
        jnp.einsum("qkgd,rkd->kgqr", queries4, key_block, preferred_element_type=jnp.float32)
        * HD ** (-0.5),
        NEGATIVE,
    )
    new_max = jnp.maximum(running_max, jnp.max(scores, axis=-1))
    weights = jnp.exp(jnp.where(allowed, scores - new_max[..., None], NEGATIVE))
    denominator = jnp.sum(weights, axis=-1)
    weighted = jnp.einsum(
        "kgqr,rkd->kgqd",
        weights.astype(jnp.bfloat16),
        value_block,
        preferred_element_type=jnp.float32,
    )
    return (weighted, new_max, denominator)


def start_state(kv_heads, per_head, tokens_dev):
    return (
        jnp.zeros((kv_heads, per_head, tokens_dev, HD), jnp.float32),
        jnp.full((kv_heads, per_head, tokens_dev), NEGATIVE, jnp.float32),
        jnp.zeros((kv_heads, per_head, tokens_dev), jnp.float32),
    )


def shards_wide(
    patches,
    route_count,
    text_states,
    segment_ids,
    vision_gain,
    merge_up,
    merge_down,
    norm_gain,
    query_weight,
    kv_weight,
):
    ctx_size = lax.axis_size("ctx")
    grp_size = lax.axis_size("grp")
    tp_size = lax.axis_size("tp")
    owner_index = lax.axis_index("ctx")
    member = lax.axis_index("grp")
    tp_index = lax.axis_index("tp")
    tensor_index = tp_index * grp_size + member
    row_count = patches.shape[0]
    bucket_rows = row_count // ctx_size
    tokens_dev = text_states.shape[0]
    grouped = patches.astype(jnp.float32).reshape(row_count, 4, -1)
    patch_normed = rms_scale(grouped, vision_gain).reshape(row_count, -1).astype(jnp.bfloat16)
    hidden = jax.nn.gelu(
        jnp.dot(patch_normed, merge_up, preferred_element_type=jnp.float32), approximate=False
    ).astype(jnp.bfloat16)
    partial_value = jnp.dot(hidden, merge_down, preferred_element_type=jnp.float32)
    column = lax.dynamic_slice_in_dim(route_count, owner_index, 1, 1)[:, 0]
    count_ends = jnp.cumsum(column)
    count_starts = count_ends - column
    slot_ids = jnp.arange(tokens_dev, dtype=jnp.int32)
    source = jnp.sum((count_ends[None, :] <= slot_ids[:, None]).astype(jnp.int32), axis=1)
    source = jnp.minimum(source, ctx_size - 1)
    source_match = source[:, None] == jnp.arange(ctx_size, dtype=jnp.int32)[None, :]
    first_slot = jnp.sum(jnp.where(source_match, count_starts[None, :], 0), axis=1)
    visual = slot_ids < count_ends[ctx_size - 1]
    pick_rows = jnp.where(visual, source * bucket_rows + slot_ids - first_slot, 0)
    merged = lax.psum(partial_value, ("tp", "grp")).astype(jnp.bfloat16)
    arrived = lax.all_to_all(
        merged.reshape(ctx_size, bucket_rows, -1), "ctx", split_axis=0, concat_axis=0, tiled=True
    )
    arrived = arrived.reshape(row_count, -1)
    text_full = lax.all_gather(text_states, ("tp", "grp"), axis=1, tiled=True)
    packed = jnp.where(visual[:, None], arrived[pick_rows], text_full)
    normal = rms_scale(packed.astype(jnp.float32), norm_gain).astype(jnp.bfloat16)
    queries = jnp.dot(normal, query_weight, preferred_element_type=jnp.float32).astype(jnp.bfloat16)
    kv_pairs = jnp.dot(normal, kv_weight, preferred_element_type=jnp.float32).astype(jnp.bfloat16)
    heads_dev = queries.shape[1] // HD
    group = HQ // KVH
    kv_per_tp = KVH // tp_size
    query_pos = owner_index * tokens_dev + slot_ids
    query_seg = segment_ids[query_pos]
    visual_count = jnp.sum(route_count, axis=0)
    kv_local = tensor_index * heads_dev // group - tp_index * kv_per_tp
    chosen = lax.dynamic_slice_in_dim(kv_pairs, kv_local * 2 * HD, 2 * HD, 1)
    queries4 = queries.reshape(tokens_dev, 1, heads_dev, HD)
    shard_piece = lax.all_gather(chosen, "ctx", axis=0, tiled=True)
    key_pos = jnp.arange(shard_piece.shape[0], dtype=jnp.int32)
    weighted, running_max, denominator = attend(
        start_state(1, heads_dev, tokens_dev),
        queries4,
        shard_piece,
        key_pos,
        query_pos,
        query_seg,
        segment_ids,
        visual_count,
        tokens_dev,
    )
    result = (weighted / denominator[..., None]).reshape(heads_dev, tokens_dev, HD)
    return result.transpose(1, 0, 2).reshape(tokens_dev, -1).astype(jnp.bfloat16)


MESH = pl.DeviceIdType.MESH
UP_CHUNKS = 4
BF16 = jnp.bfloat16
F32 = jnp.float32


def fits(mesh):
    return mesh.shape["grp"] == 2 and mesh.size <= 64


def erf(value):
    value = jnp.clip(value, -4.0, 4.0)
    square = value * value
    top = jnp.full_like(value, -2.72614225801306e-10)
    for factor in (
        2.77068142495902e-08,
        -2.10102402082508e-06,
        -5.69250639462346e-05,
        -7.34990630326855e-04,
        -2.95459980854025e-03,
        -1.60960333262415e-02,
    ):
        top = top * square + factor
    low = jnp.full_like(value, -1.45660718464996e-05)
    for factor in (
        -2.13374055278905e-04,
        -1.68282697438203e-03,
        -7.37332916720468e-03,
        -1.42647390514189e-02,
    ):
        low = low * square + factor
    return value * top / low


def remote(src, dst, send, recv, where):
    return pltpu.make_async_remote_copy(
        src_ref=src,
        dst_ref=dst,
        send_sem=send,
        recv_sem=recv,
        device_id=where,
        device_id_type=MESH,
    )


def body(
    ctx_size,
    tp_size,
    grp_size,
    kv_heads_tp,
    patches,
    route,
    text,
    seg,
    vgain,
    up,
    down,
    ngain,
    wq,
    wkv,
    out,
    up_v,
    down_v,
    wq_v,
    wkv_v,
    full,
    rs_send,
    rs_recv,
    merged,
    arrived,
    gathered,
    vis,
    normal,
    queries,
    kv_full,
    load_sem,
    own_sem,
    text_recv,
    up_send,
    down_send,
    side_send,
    rs_send_sem,
    rs_recv_sem,
    row_send,
    row_recv,
    row_own,
    vis_send,
    vis_recv,
    vis_own,
    kv_send,
    kv_recv,
):
    c = lax.axis_index("ctx")
    z = lax.axis_index("tp")
    g = lax.axis_index("grp")
    members = tp_size * grp_size
    mine = z * grp_size + g
    rows, features_in = patches.shape
    bucket = rows // ctx_size
    tokens_dev, width = text.shape
    heads_dev = wq.shape[1] // HD
    group = HQ // KVH
    vis_rows = ctx_size * bucket

    part = features_in // UP_CHUNKS
    up_loads = [
        pltpu.make_async_copy(
            up.at[pl.ds(i * part, part)], up_v.at[pl.ds(i * part, part)], load_sem.at[i]
        )
        for i in range(UP_CHUNKS)
    ]
    down_load = pltpu.make_async_copy(down, down_v, load_sem.at[UP_CHUNKS])
    kv_local = mine * heads_dev // group - z * kv_heads_tp
    kv_columns = pl.ds(pl.multiple_of(kv_local * 2 * HD, 2 * HD), 2 * HD)
    kv_load = pltpu.make_async_copy(wkv.at[:, kv_columns], wkv_v, load_sem.at[UP_CHUNKS + 1])
    q_load = pltpu.make_async_copy(wq, wq_v, load_sem.at[UP_CHUNKS + 2])
    own_text = pltpu.make_async_copy(text, full.at[mine], own_sem)
    own_text.start()
    for load in up_loads:
        load.start()
    down_load.start()
    kv_load.start()
    q_load.start()

    tensor_peers = []
    for step in range(1, members):
        other = lax.rem(mine + step, members)
        tensor_peers.append((other, {"tp": other // grp_size, "grp": lax.rem(other, grp_size)}))
    ctx_peers = []
    for step in range(1, ctx_size):
        other = lax.rem(c + step, ctx_size)
        ctx_peers.append((other, {"ctx": other}))
    barrier = pltpu.get_barrier_semaphore()
    for _, where in tensor_peers + ctx_peers:
        pl.semaphore_signal(barrier, inc=1, device_id=where, device_id_type=MESH)
    pl.semaphore_wait(barrier, len(tensor_peers) + len(ctx_peers))

    def up_copy(step):
        slot = (z - step) * grp_size + g
        src = text if step == 0 else full.at[slot]
        return remote(src, full.at[slot], up_send.at[step], text_recv.at[slot], {"tp": z + 1})

    def down_copy(step):
        slot = (z + step) * grp_size + g
        src = text if step == 0 else full.at[slot]
        return remote(src, full.at[slot], down_send.at[step], text_recv.at[slot], {"tp": z - 1})

    def side_copy(from_z, own):
        slot = from_z * grp_size + g
        src = text if own else full.at[slot]
        return remote(src, full.at[slot], side_send.at[from_z], text_recv.at[slot], {"grp": 1 - g})

    def slot_arrived(slot):
        remote(
            full.at[slot], full.at[slot], up_send.at[0], text_recv.at[slot], {"grp": 1 - g}
        ).wait_recv()

    def sends_up(step):
        return (z >= step) & (z + 1 < tp_size)

    def sends_down(step):
        return (z + step < tp_size) & (z >= 1)

    def text_step(step):
        if step == 0:
            side_now = [(z, None)]
        else:
            side_now = [(z - step, z >= step), (z + step, z + step < tp_size)]
            for from_z, there in side_now:

                @pl.when(there)
                def _():
                    slot_arrived(from_z * grp_size + g)

        if step < tp_size - 1:

            @pl.when(sends_up(step))
            def _():
                up_copy(step).start()

            @pl.when(sends_down(step))
            def _():
                down_copy(step).start()

        for from_z, there in side_now:
            if there is None:
                side_copy(from_z, True).start()
            else:

                @pl.when(there)
                def _():
                    side_copy(from_z, False).start()

    text_step(0)

    grouped = patches.shape[1] // vgain.shape[1]
    span = vgain.shape[1]
    normed = []
    for i in range(grouped):
        piece = patches[:, i * span : (i + 1) * span].astype(F32)
        scale = lax.rsqrt(jnp.mean(piece * piece, axis=-1, keepdims=True) + EPSILON)
        normed.append((piece * scale * vgain[...]).astype(BF16))
    hidden = jnp.zeros((rows, up.shape[1]), F32)
    for i in range(UP_CHUNKS):
        up_loads[i].wait()
        hidden = hidden + jnp.dot(
            normed[i], up_v[i * part : (i + 1) * part, :], preferred_element_type=F32
        )
    hidden = (0.5 * hidden * (1.0 + erf(hidden * 0.5**0.5))).astype(BF16)
    down_load.wait()
    for t in range(members):
        piece = jnp.dot(
            hidden, down_v[:, t * width : (t + 1) * width], preferred_element_type=F32
        )
        rs_send[t] = piece.astype(rs_send.dtype)

    rs_copies = []
    for i, (other, where) in enumerate(tensor_peers):
        copy = remote(
            rs_send.at[other], rs_recv.at[mine], rs_send_sem.at[i], rs_recv_sem.at[mine], where
        )
        copy.start()
        rs_copies.append(copy)
    for step in range(1, tp_size - 1):
        text_step(step)
    total = rs_send[mine].astype(F32)
    for i, (other, where) in enumerate(tensor_peers):
        remote(
            rs_send.at[other], rs_recv.at[other], rs_send_sem.at[i], rs_recv_sem.at[other], where
        ).wait_recv()
        total = total + rs_recv[other].astype(F32)
    total = total.astype(BF16).astype(merged.dtype)
    for d in range(ctx_size):
        merged[d] = total[d * bucket : (d + 1) * bucket, :]

    row_copies = []
    for i, (other, where) in enumerate(ctx_peers):
        copy = remote(
            merged.at[other], arrived.at[c], row_send.at[i], row_recv.at[c], where
        )
        copy.start()
        row_copies.append(copy)
    row_keep = pltpu.make_async_copy(merged.at[c], arrived.at[c], row_own)
    row_keep.start()
    text_step(tp_size - 1)
    row_keep.wait()
    for i, (other, where) in enumerate(ctx_peers):
        remote(
            merged.at[other], arrived.at[other], row_send.at[i], row_recv.at[other], where
        ).wait_recv()
    vis_copies = []
    for i, (other, where) in enumerate(tensor_peers):
        copy = remote(arrived, gathered.at[mine], vis_send.at[i], vis_recv.at[mine], where)
        copy.start()
        vis_copies.append(copy)
    vis_keep = pltpu.make_async_copy(arrived, gathered.at[mine], vis_own)
    vis_keep.start()

    own_text.wait()
    for t in range(members):

        @pl.when(t % grp_size != g)
        def _():
            slot_arrived(t)

    squares = jnp.zeros((tokens_dev, 1), F32)
    for t in range(members):
        piece = full[t].astype(F32)
        squares = squares + jnp.sum(piece * piece, axis=-1, keepdims=True)
    features = members * width
    scale = lax.rsqrt(squares / features + EPSILON)
    for t in range(members):
        gain = ngain[:, t * width : (t + 1) * width]
        normal[:, t * width : (t + 1) * width] = (full[t].astype(F32) * scale * gain).astype(BF16)
    kv_load.wait()
    kv_full[c] = jnp.dot(normal[...], wkv_v[...], preferred_element_type=F32).astype(BF16)
    late = -(-vis_rows // 16) * 16
    tail = pl.ds(late, tokens_dev - late)
    first = pl.ds(0, late)
    kv_copies = []

    def kv_copy(i, where, block, span_rows, phase):
        return remote(
            kv_full.at[block, span_rows],
            kv_full.at[block, span_rows],
            kv_send.at[phase, i],
            kv_recv.at[phase, block],
            where,
        )

    for i, (other, where) in enumerate(ctx_peers):
        copy = kv_copy(i, where, c, tail, 0)
        copy.start()
        kv_copies.append(copy)
    q_load.wait()
    for n in range(0, queries.shape[1], 2 * HD):
        queries[:, n : n + 2 * HD] = jnp.dot(
            normal[...], wq_v[:, n : n + 2 * HD], preferred_element_type=F32
        ).astype(BF16)

    slot_of = lax.broadcasted_iota(jnp.int32, (late, vis_rows), 0)
    row_of = lax.broadcasted_iota(jnp.int32, (late, vis_rows), 1)
    chosen = jnp.zeros((late, vis_rows), F32)
    start = jnp.int32(0)
    for source in range(ctx_size):
        count = route[source, c]
        for j in range(bucket):
            at = jnp.where(j < count, start + j, -1)
            hit = (slot_of == at) & (row_of == source * bucket + j)
            chosen = jnp.where(hit, 1.0, chosen)
        start = start + count
    chosen = chosen.astype(BF16)
    is_visual = lax.broadcasted_iota(jnp.int32, (late, 1), 0) < start

    vis_keep.wait()
    for i, (other, where) in enumerate(tensor_peers):
        remote(
            arrived, gathered.at[other], vis_send.at[i], vis_recv.at[other], where
        ).wait_recv()
    for t in range(members):
        for source in range(ctx_size):
            vis[source * bucket : (source + 1) * bucket, t * width : (t + 1) * width] = gathered[
                t, source
            ].astype(F32)
    visual = vis[...]
    scale = lax.rsqrt(jnp.mean(visual * visual, axis=-1, keepdims=True) + EPSILON)
    visual = (visual * scale * ngain[...]).astype(BF16)
    visual = jnp.dot(chosen, visual, preferred_element_type=F32).astype(BF16)
    kv_rows = jnp.dot(visual, wkv_v[...], preferred_element_type=F32).astype(BF16)
    kv_full[c, 0:late, :] = jnp.where(
        is_visual, kv_rows.astype(F32), kv_full[c, 0:late, :].astype(F32)
    ).astype(BF16)
    for i, (other, where) in enumerate(ctx_peers):
        copy = kv_copy(i, where, c, first, 1)
        copy.start()
        kv_copies.append(copy)
    for n in range(0, queries.shape[1], 2 * HD):
        query_rows = jnp.dot(visual, wq_v[:, n : n + 2 * HD], preferred_element_type=F32)
        queries[0:late, n : n + 2 * HD] = jnp.where(
            is_visual,
            query_rows.astype(BF16).astype(F32),
            queries[0:late, n : n + 2 * HD].astype(F32),
        ).astype(BF16)

    mine_row = jnp.broadcast_to(seg[pl.ds(c, 1), :], (tokens_dev, tokens_dev))
    query_seg = mine_row.T
    lane = lax.broadcasted_iota(jnp.int32, (tokens_dev, tokens_dev), 1)
    row = lax.broadcasted_iota(jnp.int32, (tokens_dev, tokens_dev), 0)
    query_pos = c * tokens_dev + row
    allowed = []
    for block in range(ctx_size):
        count = route[0, block]
        for source in range(1, ctx_size):
            count = count + route[source, block]
        near = (lane < count) | (block * tokens_dev + lane <= query_pos)
        allowed.append((query_seg == seg[block : block + 1, :]) & near)
    bias = jnp.concatenate([jnp.where(ok, 0.0, NEGATIVE) for ok in allowed], axis=1)

    for phase, span_rows in ((0, tail), (1, first)):
        for i, (other, where) in enumerate(ctx_peers):
            kv_copy(i, where, other, span_rows, phase).wait_recv()
    keys = jnp.concatenate([kv_full[b, :, :HD] for b in range(ctx_size)], axis=0)
    values = jnp.concatenate([kv_full[b, :, HD:] for b in range(ctx_size)], axis=0)
    for h in range(heads_dev):
        query = queries[:, h * HD : (h + 1) * HD]
        scores = lax.dot_general(
            query, keys, (((1,), (1,)), ((), ())), preferred_element_type=F32
        )
        scores = jnp.where(bias == 0.0, scores * HD ** (-0.5), NEGATIVE)
        weights = jnp.exp(scores - jnp.max(scores, axis=-1, keepdims=True))
        total = jnp.sum(weights, axis=-1, keepdims=True)
        mixed = jnp.dot(weights.astype(BF16), values, preferred_element_type=F32)
        out[:, h * HD : (h + 1) * HD] = (mixed / total).astype(BF16)

    for step in range(tp_size - 1):

        @pl.when(sends_up(step))
        def _():
            up_copy(step).wait_send()

        @pl.when(sends_down(step))
        def _():
            down_copy(step).wait_send()

    for from_z in range(tp_size):
        side_copy(from_z, False).wait_send()
    for copy in rs_copies + row_copies + vis_copies + kv_copies:
        copy.wait_send()


def fused(
    patches,
    route_count,
    text_states,
    segment_ids,
    vision_gain,
    merge_up,
    merge_down,
    norm_gain,
    query_weight,
    kv_weight,
):
    ctx_size = lax.axis_size("ctx")
    tp_size = lax.axis_size("tp")
    grp_size = lax.axis_size("grp")
    members = tp_size * grp_size
    rows = patches.shape[0]
    bucket = rows // ctx_size
    tokens_dev, width = text_states.shape
    features = query_weight.shape[0]
    vmem = pl.BlockSpec(memory_space=pltpu.VMEM)
    anywhere = pl.BlockSpec(memory_space=pl.ANY)
    scalars = pl.BlockSpec(memory_space=pltpu.SMEM)
    dma = pltpu.SemaphoreType.DMA
    kernel = functools.partial(body, ctx_size, tp_size, grp_size, KVH // tp_size)
    return pl.pallas_call(
        kernel,
        out_shape=jax.ShapeDtypeStruct((tokens_dev, query_weight.shape[1]), BF16),
        in_specs=[
            vmem,
            scalars,
            anywhere,
            vmem,
            vmem,
            anywhere,
            anywhere,
            vmem,
            anywhere,
            anywhere,
        ],
        out_specs=vmem,
        scratch_shapes=[
            pltpu.VMEM(merge_up.shape, BF16),
            pltpu.VMEM(merge_down.shape, BF16),
            pltpu.VMEM(query_weight.shape, BF16),
            pltpu.VMEM((features, 2 * HD), BF16),
            pltpu.VMEM((members, tokens_dev, width), BF16),
            pltpu.VMEM((members, rows, width), BF16),
            pltpu.VMEM((members, rows, width), BF16),
            pltpu.VMEM((ctx_size, bucket, width), F32),
            pltpu.VMEM((ctx_size, bucket, width), F32),
            pltpu.VMEM((members, ctx_size, bucket, width), F32),
            pltpu.VMEM((rows, features), F32),
            pltpu.VMEM((tokens_dev, features), BF16),
            pltpu.VMEM((tokens_dev, query_weight.shape[1]), BF16),
            pltpu.VMEM((ctx_size, tokens_dev, 2 * HD), BF16),
            dma((UP_CHUNKS + 3,)),
            dma,
            dma((members,)),
            dma((tp_size,)),
            dma((tp_size,)),
            dma((tp_size,)),
            dma((members,)),
            dma((members,)),
            dma((ctx_size,)),
            dma((ctx_size,)),
            dma,
            dma((members,)),
            dma((members,)),
            dma,
            dma((2, ctx_size)),
            dma((2, ctx_size)),
        ],
        compiler_params=pltpu.CompilerParams(
            collective_id=0, has_side_effects=True, vmem_limit_bytes=56 * 2**20
        ),
    )(
        patches,
        route_count,
        text_states,
        segment_ids.reshape(ctx_size, tokens_dev),
        vision_gain.reshape(1, -1),
        merge_up,
        merge_down,
        norm_gain.reshape(1, -1),
        query_weight,
        kv_weight,
    )


def solution(mesh):
    return jax.shard_map(
        fused if fits(mesh) else shards_wide,
        mesh=mesh,
        in_specs=(
            P("ctx", None),
            P(),
            P("ctx", ("tp", "grp")),
            P(),
            P(),
            P(None, ("tp", "grp")),
            P(("tp", "grp"), None),
            P(),
            P(None, ("tp", "grp")),
            P(None, "tp"),
        ),
        out_specs=P("ctx", ("tp", "grp")),
        check_vma=False,
    )
```

```python
import functools

import jax
import jax.numpy as jnp
from jax import lax
from jax.experimental import pallas as pl
from jax.experimental.pallas import tpu as pltpu
from jax.sharding import PartitionSpec as P

HQ = 32
KVH = 8
HD = 128


EPSILON = 1e-06
NEGATIVE = -1e30


def rms_scale(values, gain):
    mean_square = jnp.mean(values * values, axis=-1, keepdims=True)
    return values * lax.rsqrt(mean_square + EPSILON) * gain


def attend(
    running,
    queries4,
    shard_piece,
    key_pos,
    query_pos,
    query_seg,
    segment_ids,
    visual_count,
    tokens_dev,
):
    weighted, running_max, denominator = running
    piece_rows = shard_piece.shape[0]
    kv_heads = queries4.shape[1]
    kv_split = shard_piece.reshape(piece_rows, kv_heads, 2, HD)
    key_block = kv_split[:, :, 0]
    value_block = kv_split[:, :, 1]
    key_owner = key_pos // tokens_dev
    owner_match = key_owner[:, None] == jnp.arange(visual_count.shape[0], dtype=jnp.int32)[None, :]
    visual_limit = jnp.sum(jnp.where(owner_match, visual_count[None, :], 0), axis=1)
    key_visual = key_pos % tokens_dev < visual_limit
    key_seg = segment_ids[key_pos]
    allowed = (query_seg[:, None] == key_seg[None, :]) & (
        key_visual[None, :] | (key_pos[None, :] <= query_pos[:, None])
    )
    scores = jnp.where(
        allowed,
        jnp.einsum("qkgd,rkd->kgqr", queries4, key_block, preferred_element_type=jnp.float32)
        * HD ** (-0.5),
        NEGATIVE,
    )
    new_max = jnp.maximum(running_max, jnp.max(scores, axis=-1))
    weights = jnp.exp(jnp.where(allowed, scores - new_max[..., None], NEGATIVE))
    denominator = jnp.sum(weights, axis=-1)
    weighted = jnp.einsum(
        "kgqr,rkd->kgqd",
        weights.astype(jnp.bfloat16),
        value_block,
        preferred_element_type=jnp.float32,
    )
    return (weighted, new_max, denominator)


def start_state(kv_heads, per_head, tokens_dev):
    return (
        jnp.zeros((kv_heads, per_head, tokens_dev, HD), jnp.float32),
        jnp.full((kv_heads, per_head, tokens_dev), NEGATIVE, jnp.float32),
        jnp.zeros((kv_heads, per_head, tokens_dev), jnp.float32),
    )


def shards_wide(
    patches,
    route_count,
    text_states,
    segment_ids,
    vision_gain,
    merge_up,
    merge_down,
    norm_gain,
    query_weight,
    kv_weight,
):
    ctx_size = lax.axis_size("ctx")
    grp_size = lax.axis_size("grp")
    tp_size = lax.axis_size("tp")
    owner_index = lax.axis_index("ctx")
    member = lax.axis_index("grp")
    tp_index = lax.axis_index("tp")
    tensor_index = tp_index * grp_size + member
    row_count = patches.shape[0]
    bucket_rows = row_count // ctx_size
    tokens_dev = text_states.shape[0]
    grouped = patches.astype(jnp.float32).reshape(row_count, 4, -1)
    patch_normed = rms_scale(grouped, vision_gain).reshape(row_count, -1).astype(jnp.bfloat16)
    hidden = jax.nn.gelu(
        jnp.dot(patch_normed, merge_up, preferred_element_type=jnp.float32), approximate=False
    ).astype(jnp.bfloat16)
    partial_value = jnp.dot(hidden, merge_down, preferred_element_type=jnp.float32)
    column = lax.dynamic_slice_in_dim(route_count, owner_index, 1, 1)[:, 0]
    count_ends = jnp.cumsum(column)
    count_starts = count_ends - column
    slot_ids = jnp.arange(tokens_dev, dtype=jnp.int32)
    source = jnp.sum((count_ends[None, :] <= slot_ids[:, None]).astype(jnp.int32), axis=1)
    source = jnp.minimum(source, ctx_size - 1)
    source_match = source[:, None] == jnp.arange(ctx_size, dtype=jnp.int32)[None, :]
    first_slot = jnp.sum(jnp.where(source_match, count_starts[None, :], 0), axis=1)
    visual = slot_ids < count_ends[ctx_size - 1]
    pick_rows = jnp.where(visual, source * bucket_rows + slot_ids - first_slot, 0)
    merged = lax.psum(partial_value, ("tp", "grp")).astype(jnp.bfloat16)
    arrived = lax.all_to_all(
        merged.reshape(ctx_size, bucket_rows, -1), "ctx", split_axis=0, concat_axis=0, tiled=True
    )
    arrived = arrived.reshape(row_count, -1)
    text_full = lax.all_gather(text_states, ("tp", "grp"), axis=1, tiled=True)
    packed = jnp.where(visual[:, None], arrived[pick_rows], text_full)
    normal = rms_scale(packed.astype(jnp.float32), norm_gain).astype(jnp.bfloat16)
    queries = jnp.dot(normal, query_weight, preferred_element_type=jnp.float32).astype(jnp.bfloat16)
    kv_pairs = jnp.dot(normal, kv_weight, preferred_element_type=jnp.float32).astype(jnp.bfloat16)
    heads_dev = queries.shape[1] // HD
    group = HQ // KVH
    kv_per_tp = KVH // tp_size
    query_pos = owner_index * tokens_dev + slot_ids
    query_seg = segment_ids[query_pos]
    visual_count = jnp.sum(route_count, axis=0)
    kv_local = tensor_index * heads_dev // group - tp_index * kv_per_tp
    chosen = lax.dynamic_slice_in_dim(kv_pairs, kv_local * 2 * HD, 2 * HD, 1)
    queries4 = queries.reshape(tokens_dev, 1, heads_dev, HD)
    shard_piece = lax.all_gather(chosen, "ctx", axis=0, tiled=True)
    key_pos = jnp.arange(shard_piece.shape[0], dtype=jnp.int32)
    weighted, running_max, denominator = attend(
        start_state(1, heads_dev, tokens_dev),
        queries4,
        shard_piece,
        key_pos,
        query_pos,
        query_seg,
        segment_ids,
        visual_count,
        tokens_dev,
    )
    result = (weighted / denominator[..., None]).reshape(heads_dev, tokens_dev, HD)
    return result.transpose(1, 0, 2).reshape(tokens_dev, -1).astype(jnp.bfloat16)


MESH = pl.DeviceIdType.MESH
BF16 = jnp.bfloat16
F32 = jnp.float32


def fits(mesh):
    return mesh.shape["grp"] == 2 and mesh.size <= 64


def erf(value):
    value = jnp.clip(value, -4.0, 4.0)
    square = value * value
    top = jnp.full_like(value, -2.72614225801306e-10)
    for factor in (
        2.77068142495902e-08,
        -2.10102402082508e-06,
        -5.69250639462346e-05,
        -7.34990630326855e-04,
        -2.95459980854025e-03,
        -1.60960333262415e-02,
    ):
        top = top * square + factor
    low = jnp.full_like(value, -1.45660718464996e-05)
    for factor in (
        -2.13374055278905e-04,
        -1.68282697438203e-03,
        -7.37332916720468e-03,
        -1.42647390514189e-02,
    ):
        low = low * square + factor
    return value * top / low


def remote(src, dst, send, recv, where):
    return pltpu.make_async_remote_copy(
        src_ref=src,
        dst_ref=dst,
        send_sem=send,
        recv_sem=recv,
        device_id=where,
        device_id_type=MESH,
    )


def body(
    ctx_size,
    tp_size,
    grp_size,
    kv_heads_tp,
    patches,
    route,
    text,
    seg,
    vgain,
    up,
    down,
    ngain,
    wq,
    wkv,
    out,
    up_v,
    down_v,
    wq_v,
    wkv_v,
    full,
    rs_send,
    rs_recv,
    merged,
    arrived,
    gathered,
    vis,
    normal,
    queries,
    kv_full,
    load_sem,
    own_sem,
    text_recv,
    up_send,
    down_send,
    side_send,
    rs_send_sem,
    rs_recv_sem,
    row_send,
    row_recv,
    row_own,
    vis_send,
    vis_recv,
    vis_own,
    kv_send,
    kv_recv,
):
    c = lax.axis_index("ctx")
    z = lax.axis_index("tp")
    g = lax.axis_index("grp")
    members = tp_size * grp_size
    mine = z * grp_size + g
    rows, features_in = patches.shape
    bucket = rows // ctx_size
    tokens_dev, width = text.shape
    heads_dev = wq.shape[1] // HD
    group = HQ // KVH
    vis_rows = ctx_size * bucket

    tensor_peers = []
    for step in range(1, members):
        other = lax.rem(mine + step, members)
        tensor_peers.append((other, {"tp": other // grp_size, "grp": lax.rem(other, grp_size)}))
    ctx_peers = []
    for step in range(1, ctx_size):
        other = lax.rem(c + step, ctx_size)
        ctx_peers.append((other, {"ctx": other}))
    barrier = pltpu.get_barrier_semaphore()
    for _, where in tensor_peers + ctx_peers:
        pl.semaphore_signal(barrier, inc=1, device_id=where, device_id_type=MESH)

    span = vgain.shape[0] * vgain.shape[1]
    up_chunks = features_in // span
    up_loads = [
        pltpu.make_async_copy(
            up.at[:, pl.ds(i * span, span)], up_v.at[:, pl.ds(i * span, span)], load_sem.at[i]
        )
        for i in range(up_chunks)
    ]
    down_load = pltpu.make_async_copy(down, down_v, load_sem.at[up_chunks])
    kv_local = mine * heads_dev // group - z * kv_heads_tp
    kv_columns = pl.ds(pl.multiple_of(kv_local * 2 * HD, 2 * HD), 2 * HD)
    kv_load = pltpu.make_async_copy(wkv.at[:, kv_columns], wkv_v, load_sem.at[up_chunks + 1])
    q_load = pltpu.make_async_copy(wq, wq_v, load_sem.at[up_chunks + 2])
    own_text = pltpu.make_async_copy(text, full.at[mine], own_sem)
    own_text.start()
    for load in up_loads:
        load.start()
    down_load.start()
    kv_load.start()
    q_load.start()

    pl.semaphore_wait(barrier, len(tensor_peers) + len(ctx_peers))

    def up_copy(step):
        slot = (z - step) * grp_size + g
        src = text if step == 0 else full.at[slot]
        return remote(src, full.at[slot], up_send.at[step], text_recv.at[slot], {"tp": z + 1})

    def down_copy(step):
        slot = (z + step) * grp_size + g
        src = text if step == 0 else full.at[slot]
        return remote(src, full.at[slot], down_send.at[step], text_recv.at[slot], {"tp": z - 1})

    def side_copy(from_z, own):
        slot = from_z * grp_size + g
        src = text if own else full.at[slot]
        return remote(src, full.at[slot], side_send.at[from_z], text_recv.at[slot], {"grp": 1 - g})

    def slot_arrived(slot):
        remote(
            full.at[slot], full.at[slot], up_send.at[0], text_recv.at[slot], {"grp": 1 - g}
        ).wait_recv()

    def sends_up(step):
        return (z >= step) & (z + 1 < tp_size)

    def sends_down(step):
        return (z + step < tp_size) & (z >= 1)

    def text_step(step):
        if step == 0:
            side_now = [(z, None)]
        else:
            side_now = [(z - step, z >= step), (z + step, z + step < tp_size)]
            for from_z, there in side_now:

                @pl.when(there)
                def _():
                    slot_arrived(from_z * grp_size + g)

        if step < tp_size - 1:

            @pl.when(sends_up(step))
            def _():
                up_copy(step).start()

            @pl.when(sends_down(step))
            def _():
                down_copy(step).start()

        for from_z, there in side_now:
            if there is None:
                side_copy(from_z, True).start()
            else:

                @pl.when(there)
                def _():
                    side_copy(from_z, False).start()

    text_step(0)

    gain = jnp.concatenate([vgain[i : i + 1, :] for i in range(vgain.shape[0])], axis=1)
    normed = []
    for i in range(up_chunks):
        piece = patches[:, i * span : (i + 1) * span].astype(F32)
        scale = lax.rsqrt(jnp.mean(piece * piece, axis=-1, keepdims=True) + EPSILON)
        normed.append((piece * scale * gain).astype(BF16))
    hidden = jnp.zeros((rows, up.shape[0]), F32)
    for i in range(up_chunks):
        up_loads[i].wait()
        hidden = hidden + lax.dot_general(
            normed[i],
            up_v[:, i * span : (i + 1) * span],
            (((1,), (1,)), ((), ())),
            preferred_element_type=F32,
        )
    hidden = (0.5 * hidden * (1.0 + erf(hidden * 0.5**0.5))).astype(BF16)
    down_load.wait()
    for t in range(members):
        piece = jnp.dot(
            hidden, down_v[:, t * width : (t + 1) * width], preferred_element_type=F32
        )
        rs_send[t] = piece.astype(rs_send.dtype)

    rs_copies = []
    for i, (other, where) in enumerate(tensor_peers):
        copy = remote(
            rs_send.at[other], rs_recv.at[mine], rs_send_sem.at[i], rs_recv_sem.at[mine], where
        )
        copy.start()
        rs_copies.append(copy)
    for step in range(1, tp_size - 1):
        text_step(step)
    total = rs_send[mine].astype(F32)
    for i, (other, where) in enumerate(tensor_peers):
        remote(
            rs_send.at[other], rs_recv.at[other], rs_send_sem.at[i], rs_recv_sem.at[other], where
        ).wait_recv()
        total = total + rs_recv[other].astype(F32)
    total = total.astype(BF16).astype(merged.dtype)
    for d in range(ctx_size):
        merged[d] = total[d * bucket : (d + 1) * bucket, :]

    row_copies = []
    for i, (other, where) in enumerate(ctx_peers):
        copy = remote(
            merged.at[other], arrived.at[c], row_send.at[i], row_recv.at[c], where
        )
        copy.start()
        row_copies.append(copy)
    row_keep = pltpu.make_async_copy(merged.at[c], arrived.at[c], row_own)
    row_keep.start()
    text_step(tp_size - 1)
    row_keep.wait()
    for i, (other, where) in enumerate(ctx_peers):
        remote(
            merged.at[other], arrived.at[other], row_send.at[i], row_recv.at[other], where
        ).wait_recv()
    vis_copies = []
    for i, (other, where) in enumerate(tensor_peers):
        copy = remote(arrived, gathered.at[mine], vis_send.at[i], vis_recv.at[mine], where)
        copy.start()
        vis_copies.append(copy)
    vis_keep = pltpu.make_async_copy(arrived, gathered.at[mine], vis_own)
    vis_keep.start()

    own_text.wait()
    for t in range(members):

        @pl.when(t % grp_size != g)
        def _():
            slot_arrived(t)

    squares = jnp.zeros((tokens_dev, 1), F32)
    for t in range(members):
        piece = full[t].astype(F32)
        squares = squares + jnp.sum(piece * piece, axis=-1, keepdims=True)
    features = members * width
    scale = lax.rsqrt(squares / features + EPSILON)
    for t in range(members):
        gain = ngain[:, t * width : (t + 1) * width]
        normal[:, t * width : (t + 1) * width] = (full[t].astype(F32) * scale * gain).astype(BF16)
    kv_load.wait()
    kv_full[c] = jnp.dot(normal[...], wkv_v[...], preferred_element_type=F32).astype(BF16)
    late = -(-vis_rows // 16) * 16
    tail = pl.ds(late, tokens_dev - late)
    first = pl.ds(0, late)
    kv_copies = []

    def kv_copy(i, where, block, span_rows, phase):
        return remote(
            kv_full.at[block, span_rows],
            kv_full.at[block, span_rows],
            kv_send.at[phase, i],
            kv_recv.at[phase, block],
            where,
        )

    for i, (other, where) in enumerate(ctx_peers):
        copy = kv_copy(i, where, c, tail, 0)
        copy.start()
        kv_copies.append(copy)
    q_load.wait()
    for n in range(0, queries.shape[1], 2 * HD):
        queries[:, n : n + 2 * HD] = jnp.dot(
            normal[...], wq_v[:, n : n + 2 * HD], preferred_element_type=F32
        ).astype(BF16)

    slot_of = lax.broadcasted_iota(jnp.int32, (late, vis_rows), 0)
    row_of = lax.broadcasted_iota(jnp.int32, (late, vis_rows), 1)
    chosen = jnp.zeros((late, vis_rows), F32)
    start = jnp.int32(0)
    for source in range(ctx_size):
        count = route[source, c]
        for j in range(bucket):
            at = jnp.where(j < count, start + j, -1)
            hit = (slot_of == at) & (row_of == source * bucket + j)
            chosen = jnp.where(hit, 1.0, chosen)
        start = start + count
    chosen = chosen.astype(BF16)
    is_visual = lax.broadcasted_iota(jnp.int32, (late, 1), 0) < start

    vis_keep.wait()
    for i, (other, where) in enumerate(tensor_peers):
        remote(
            arrived, gathered.at[other], vis_send.at[i], vis_recv.at[other], where
        ).wait_recv()
    for t in range(members):
        for source in range(ctx_size):
            vis[source * bucket : (source + 1) * bucket, t * width : (t + 1) * width] = gathered[
                t, source
            ].astype(F32)
    visual = vis[...]
    scale = lax.rsqrt(jnp.mean(visual * visual, axis=-1, keepdims=True) + EPSILON)
    visual = (visual * scale * ngain[...]).astype(BF16)
    visual = jnp.dot(chosen, visual, preferred_element_type=F32).astype(BF16)
    kv_rows = jnp.dot(visual, wkv_v[...], preferred_element_type=F32).astype(BF16)
    kv_full[c, 0:late, :] = jnp.where(
        is_visual, kv_rows.astype(F32), kv_full[c, 0:late, :].astype(F32)
    ).astype(BF16)
    for i, (other, where) in enumerate(ctx_peers):
        copy = kv_copy(i, where, c, first, 1)
        copy.start()
        kv_copies.append(copy)
    for n in range(0, queries.shape[1], 2 * HD):
        query_rows = jnp.dot(visual, wq_v[:, n : n + 2 * HD], preferred_element_type=F32)
        queries[0:late, n : n + 2 * HD] = jnp.where(
            is_visual,
            query_rows.astype(BF16).astype(F32),
            queries[0:late, n : n + 2 * HD].astype(F32),
        ).astype(BF16)

    mine_row = jnp.broadcast_to(seg[pl.ds(c, 1), :], (tokens_dev, tokens_dev))
    query_seg = mine_row.T
    lane = lax.broadcasted_iota(jnp.int32, (tokens_dev, tokens_dev), 1)
    row = lax.broadcasted_iota(jnp.int32, (tokens_dev, tokens_dev), 0)
    query_pos = c * tokens_dev + row
    allowed = []
    for block in range(ctx_size):
        count = route[0, block]
        for source in range(1, ctx_size):
            count = count + route[source, block]
        near = (lane < count) | (block * tokens_dev + lane <= query_pos)
        allowed.append((query_seg == seg[block : block + 1, :]) & near)
    bias = jnp.concatenate([jnp.where(ok, 0.0, NEGATIVE) for ok in allowed], axis=1)

    for phase, span_rows in ((0, tail), (1, first)):
        for i, (other, where) in enumerate(ctx_peers):
            kv_copy(i, where, other, span_rows, phase).wait_recv()
    keys = jnp.concatenate([kv_full[b, :, :HD] for b in range(ctx_size)], axis=0)
    values = jnp.concatenate([kv_full[b, :, HD:] for b in range(ctx_size)], axis=0)
    for h in range(heads_dev):
        query = queries[:, h * HD : (h + 1) * HD]
        scores = lax.dot_general(
            query, keys, (((1,), (1,)), ((), ())), preferred_element_type=F32
        )
        scores = jnp.where(bias == 0.0, scores * HD ** (-0.5), NEGATIVE)
        weights = jnp.exp(scores - jnp.max(scores, axis=-1, keepdims=True))
        total = jnp.sum(weights, axis=-1, keepdims=True)
        mixed = jnp.dot(weights.astype(BF16), values, preferred_element_type=F32)
        out[:, h * HD : (h + 1) * HD] = (mixed / total).astype(BF16)

    for step in range(tp_size - 1):

        @pl.when(sends_up(step))
        def _():
            up_copy(step).wait_send()

        @pl.when(sends_down(step))
        def _():
            down_copy(step).wait_send()

    for from_z in range(tp_size):
        side_copy(from_z, False).wait_send()
    for copy in rs_copies + row_copies + vis_copies + kv_copies:
        copy.wait_send()


def fused(
    patches,
    route_count,
    text_states,
    segment_ids,
    vision_gain,
    merge_up,
    merge_down,
    norm_gain,
    query_weight,
    kv_weight,
):
    ctx_size = lax.axis_size("ctx")
    tp_size = lax.axis_size("tp")
    grp_size = lax.axis_size("grp")
    members = tp_size * grp_size
    rows = patches.shape[0]
    bucket = rows // ctx_size
    tokens_dev, width = text_states.shape
    features = query_weight.shape[0]
    vmem = pl.BlockSpec(memory_space=pltpu.VMEM)
    anywhere = pl.BlockSpec(memory_space=pl.ANY)
    scalars = pl.BlockSpec(memory_space=pltpu.SMEM)
    dma = pltpu.SemaphoreType.DMA
    kernel = functools.partial(body, ctx_size, tp_size, grp_size, KVH // tp_size)
    return pl.pallas_call(
        kernel,
        out_shape=pltpu.VMEM((tokens_dev, query_weight.shape[1]), BF16),
        in_specs=[
            vmem,
            scalars,
            anywhere,
            vmem,
            vmem,
            anywhere,
            anywhere,
            vmem,
            anywhere,
            anywhere,
        ],
        out_specs=vmem,
        scratch_shapes=[
            pltpu.VMEM(merge_up.shape[::-1], BF16),
            pltpu.VMEM(merge_down.shape, BF16),
            pltpu.VMEM(query_weight.shape, BF16),
            pltpu.VMEM((features, 2 * HD), BF16),
            pltpu.VMEM((members, tokens_dev, width), BF16),
            pltpu.VMEM((members, rows, width), BF16),
            pltpu.VMEM((members, rows, width), BF16),
            pltpu.VMEM((ctx_size, bucket, width), F32),
            pltpu.VMEM((ctx_size, bucket, width), F32),
            pltpu.VMEM((members, ctx_size, bucket, width), F32),
            pltpu.VMEM((rows, features), F32),
            pltpu.VMEM((tokens_dev, features), BF16),
            pltpu.VMEM((tokens_dev, query_weight.shape[1]), BF16),
            pltpu.VMEM((ctx_size, tokens_dev, 2 * HD), BF16),
            dma((patches.shape[1] // vision_gain.shape[0] + 3,)),
            dma,
            dma((members,)),
            dma((tp_size,)),
            dma((tp_size,)),
            dma((tp_size,)),
            dma((members,)),
            dma((members,)),
            dma((ctx_size,)),
            dma((ctx_size,)),
            dma,
            dma((members,)),
            dma((members,)),
            dma,
            dma((2, ctx_size)),
            dma((2, ctx_size)),
        ],
        compiler_params=pltpu.CompilerParams(
            collective_id=0, has_side_effects=True, vmem_limit_bytes=56 * 2**20
        ),
    )(
        patches,
        route_count,
        text_states,
        segment_ids.reshape(ctx_size, tokens_dev),
        vision_gain.reshape(-1, HD),
        merge_up.T,
        merge_down,
        norm_gain.reshape(1, -1),
        query_weight,
        kv_weight,
    )


def solution(mesh):
    return jax.shard_map(
        fused if fits(mesh) else shards_wide,
        mesh=mesh,
        in_specs=(
            P("ctx", None),
            P(),
            P("ctx", ("tp", "grp")),
            P(),
            P(),
            P(None, ("tp", "grp")),
            P(("tp", "grp"), None),
            P(),
            P(None, ("tp", "grp")),
            P(None, "tp"),
        ),
        out_specs=P("ctx", ("tp", "grp")),
        check_vma=False,
    )
```

```python
import functools

import jax
import jax.numpy as jnp
from jax import lax
from jax.experimental import pallas as pl
from jax.experimental.pallas import tpu as pltpu
from jax.sharding import PartitionSpec as P

HQ = 32
KVH = 8
HD = 128


EPSILON = 1e-06
NEGATIVE = -1e30


def rms_scale(values, gain):
    mean_square = jnp.mean(values * values, axis=-1, keepdims=True)
    return values * lax.rsqrt(mean_square + EPSILON) * gain


def attend(
    running,
    queries4,
    shard_piece,
    key_pos,
    query_pos,
    query_seg,
    segment_ids,
    visual_count,
    tokens_dev,
):
    weighted, running_max, denominator = running
    piece_rows = shard_piece.shape[0]
    kv_heads = queries4.shape[1]
    kv_split = shard_piece.reshape(piece_rows, kv_heads, 2, HD)
    key_block = kv_split[:, :, 0]
    value_block = kv_split[:, :, 1]
    key_owner = key_pos // tokens_dev
    owner_match = key_owner[:, None] == jnp.arange(visual_count.shape[0], dtype=jnp.int32)[None, :]
    visual_limit = jnp.sum(jnp.where(owner_match, visual_count[None, :], 0), axis=1)
    key_visual = key_pos % tokens_dev < visual_limit
    key_seg = segment_ids[key_pos]
    allowed = (query_seg[:, None] == key_seg[None, :]) & (
        key_visual[None, :] | (key_pos[None, :] <= query_pos[:, None])
    )
    scores = jnp.where(
        allowed,
        jnp.einsum("qkgd,rkd->kgqr", queries4, key_block, preferred_element_type=jnp.float32)
        * HD ** (-0.5),
        NEGATIVE,
    )
    new_max = jnp.maximum(running_max, jnp.max(scores, axis=-1))
    weights = jnp.exp(jnp.where(allowed, scores - new_max[..., None], NEGATIVE))
    denominator = jnp.sum(weights, axis=-1)
    weighted = jnp.einsum(
        "kgqr,rkd->kgqd",
        weights.astype(jnp.bfloat16),
        value_block,
        preferred_element_type=jnp.float32,
    )
    return (weighted, new_max, denominator)


def start_state(kv_heads, per_head, tokens_dev):
    return (
        jnp.zeros((kv_heads, per_head, tokens_dev, HD), jnp.float32),
        jnp.full((kv_heads, per_head, tokens_dev), NEGATIVE, jnp.float32),
        jnp.zeros((kv_heads, per_head, tokens_dev), jnp.float32),
    )


def shards_wide(
    patches,
    route_count,
    text_states,
    segment_ids,
    vision_gain,
    merge_up,
    merge_down,
    norm_gain,
    query_weight,
    kv_weight,
):
    ctx_size = lax.axis_size("ctx")
    grp_size = lax.axis_size("grp")
    tp_size = lax.axis_size("tp")
    owner_index = lax.axis_index("ctx")
    member = lax.axis_index("grp")
    tp_index = lax.axis_index("tp")
    tensor_index = tp_index * grp_size + member
    row_count = patches.shape[0]
    bucket_rows = row_count // ctx_size
    tokens_dev = text_states.shape[0]
    grouped = patches.astype(jnp.float32).reshape(row_count, 4, -1)
    patch_normed = rms_scale(grouped, vision_gain).reshape(row_count, -1).astype(jnp.bfloat16)
    hidden = jax.nn.gelu(
        jnp.dot(patch_normed, merge_up, preferred_element_type=jnp.float32), approximate=False
    ).astype(jnp.bfloat16)
    partial_value = jnp.dot(hidden, merge_down, preferred_element_type=jnp.float32)
    column = lax.dynamic_slice_in_dim(route_count, owner_index, 1, 1)[:, 0]
    count_ends = jnp.cumsum(column)
    count_starts = count_ends - column
    slot_ids = jnp.arange(tokens_dev, dtype=jnp.int32)
    source = jnp.sum((count_ends[None, :] <= slot_ids[:, None]).astype(jnp.int32), axis=1)
    source = jnp.minimum(source, ctx_size - 1)
    source_match = source[:, None] == jnp.arange(ctx_size, dtype=jnp.int32)[None, :]
    first_slot = jnp.sum(jnp.where(source_match, count_starts[None, :], 0), axis=1)
    visual = slot_ids < count_ends[ctx_size - 1]
    pick_rows = jnp.where(visual, source * bucket_rows + slot_ids - first_slot, 0)
    merged = lax.psum(partial_value, ("tp", "grp")).astype(jnp.bfloat16)
    arrived = lax.all_to_all(
        merged.reshape(ctx_size, bucket_rows, -1), "ctx", split_axis=0, concat_axis=0, tiled=True
    )
    arrived = arrived.reshape(row_count, -1)
    text_full = lax.all_gather(text_states, ("tp", "grp"), axis=1, tiled=True)
    packed = jnp.where(visual[:, None], arrived[pick_rows], text_full)
    normal = rms_scale(packed.astype(jnp.float32), norm_gain).astype(jnp.bfloat16)
    queries = jnp.dot(normal, query_weight, preferred_element_type=jnp.float32).astype(jnp.bfloat16)
    kv_pairs = jnp.dot(normal, kv_weight, preferred_element_type=jnp.float32).astype(jnp.bfloat16)
    heads_dev = queries.shape[1] // HD
    group = HQ // KVH
    kv_per_tp = KVH // tp_size
    query_pos = owner_index * tokens_dev + slot_ids
    query_seg = segment_ids[query_pos]
    visual_count = jnp.sum(route_count, axis=0)
    kv_local = tensor_index * heads_dev // group - tp_index * kv_per_tp
    chosen = lax.dynamic_slice_in_dim(kv_pairs, kv_local * 2 * HD, 2 * HD, 1)
    queries4 = queries.reshape(tokens_dev, 1, heads_dev, HD)
    shard_piece = lax.all_gather(chosen, "ctx", axis=0, tiled=True)
    key_pos = jnp.arange(shard_piece.shape[0], dtype=jnp.int32)
    weighted, running_max, denominator = attend(
        start_state(1, heads_dev, tokens_dev),
        queries4,
        shard_piece,
        key_pos,
        query_pos,
        query_seg,
        segment_ids,
        visual_count,
        tokens_dev,
    )
    result = (weighted / denominator[..., None]).reshape(heads_dev, tokens_dev, HD)
    return result.transpose(1, 0, 2).reshape(tokens_dev, -1).astype(jnp.bfloat16)


MESH = pl.DeviceIdType.MESH
BF16 = jnp.bfloat16
F32 = jnp.float32
HALVES = 2


def fits(mesh):
    return mesh.shape["grp"] == 2 and mesh.shape["tp"] > 2 and mesh.size <= 64


def erf(value):
    value = jnp.clip(value, -4.0, 4.0)
    square = value * value
    top = jnp.full_like(value, -2.72614225801306e-10)
    for factor in (
        2.77068142495902e-08,
        -2.10102402082508e-06,
        -5.69250639462346e-05,
        -7.34990630326855e-04,
        -2.95459980854025e-03,
        -1.60960333262415e-02,
    ):
        top = top * square + factor
    low = jnp.full_like(value, -1.45660718464996e-05)
    for factor in (
        -2.13374055278905e-04,
        -1.68282697438203e-03,
        -7.37332916720468e-03,
        -1.42647390514189e-02,
    ):
        low = low * square + factor
    return value * top / low


def remote(src, dst, send, recv, where):
    return pltpu.make_async_remote_copy(
        src_ref=src,
        dst_ref=dst,
        send_sem=send,
        recv_sem=recv,
        device_id=where,
        device_id_type=MESH,
    )


def body(
    ctx_size,
    tp_size,
    grp_size,
    kv_heads_tp,
    patches,
    route,
    text,
    seg,
    vgain,
    up,
    down,
    ngain,
    wq,
    wkv,
    out,
    up_v,
    down_v,
    wq_v,
    wkv_v,
    full,
    rs_send,
    rs_recv,
    merged,
    arrived,
    gathered,
    vis_mine,
    vis_send_rows,
    kv_sum,
    q_sum,
    queries,
    kv_full,
    load_sem,
    own_sem,
    text_recv,
    up_send,
    down_send,
    side_send,
    rs_send_sem,
    rs_recv_sem,
    row_send,
    row_recv,
    row_own,
    vis_send,
    vis_recv,
    kv_send,
    kv_recv,
):
    c = lax.axis_index("ctx")
    z = lax.axis_index("tp")
    g = lax.axis_index("grp")
    members = tp_size * grp_size
    mine = z * grp_size + g
    rows, features_in = patches.shape
    bucket = rows // ctx_size
    tokens_dev, width = text.shape
    heads_dev = wq.shape[1] // HD
    group = HQ // KVH
    vis_rows = ctx_size * bucket

    tensor_peers = []
    for step in range(1, members):
        other = lax.rem(mine + step, members)
        tensor_peers.append((other, {"tp": other // grp_size, "grp": lax.rem(other, grp_size)}))
    ctx_peers = []
    for step in range(1, ctx_size):
        other = lax.rem(c + step, ctx_size)
        ctx_peers.append((other, {"ctx": other}))
    barrier = pltpu.get_barrier_semaphore()
    for _, where in tensor_peers + ctx_peers:
        pl.semaphore_signal(barrier, inc=1, device_id=where, device_id_type=MESH)

    span = vgain.shape[0] * vgain.shape[1]
    up_chunks = features_in // span
    up_loads = [
        pltpu.make_async_copy(
            up.at[:, pl.ds(i * span, span)], up_v.at[:, pl.ds(i * span, span)], load_sem.at[i]
        )
        for i in range(up_chunks)
    ]
    down_load = pltpu.make_async_copy(down, down_v, load_sem.at[up_chunks])
    kv_local = mine * heads_dev // group - z * kv_heads_tp
    kv_columns = pl.ds(pl.multiple_of(kv_local * 2 * HD, 2 * HD), 2 * HD)
    kv_load = pltpu.make_async_copy(wkv.at[:, kv_columns], wkv_v, load_sem.at[up_chunks + 1])
    q_load = pltpu.make_async_copy(wq, wq_v, load_sem.at[up_chunks + 2])
    own_text = pltpu.make_async_copy(text, full.at[mine], own_sem)
    own_text.start()
    for load in up_loads:
        load.start()
    down_load.start()
    kv_load.start()
    q_load.start()

    gain = jnp.concatenate([vgain[i : i + 1, :] for i in range(vgain.shape[0])], axis=1)
    normed = []
    for i in range(up_chunks):
        piece = patches[:, i * span : (i + 1) * span].astype(F32)
        scale = lax.rsqrt(jnp.mean(piece * piece, axis=-1, keepdims=True) + EPSILON)
        normed.append((piece * scale * gain).astype(BF16))
    hidden = jnp.zeros((rows, up.shape[0]), F32)
    for i in range(up_chunks):
        up_loads[i].wait()
        hidden = hidden + lax.dot_general(
            normed[i],
            up_v[:, i * span : (i + 1) * span],
            (((1,), (1,)), ((), ())),
            preferred_element_type=F32,
        )
    hidden = (0.5 * hidden * (1.0 + erf(hidden * 0.5**0.5))).astype(BF16)
    down_load.wait()
    for t in range(members):
        piece = jnp.dot(
            hidden, down_v[:, t * width : (t + 1) * width], preferred_element_type=F32
        )
        rs_send[t] = piece.astype(rs_send.dtype)

    pl.semaphore_wait(barrier, len(tensor_peers) + len(ctx_peers))

    half_rows = tokens_dev // HALVES

    def part_of(half):
        return pl.ds(half * half_rows, half_rows)

    def text_copy(slot, half, own, send, where):
        src = text if own else full.at[slot]
        return remote(
            src.at[part_of(half)],
            full.at[slot, part_of(half)],
            send,
            text_recv.at[slot, half],
            where,
        )

    def up_copy(step, half):
        slot = (z - step) * grp_size + g
        return text_copy(slot, half, step == 0, up_send.at[step, half], {"tp": z + 1})

    def down_copy(step, half):
        slot = (z + step) * grp_size + g
        return text_copy(slot, half, step == 0, down_send.at[step, half], {"tp": z - 1})

    def side_copy(from_z, half, own):
        slot = from_z * grp_size + g
        return text_copy(slot, half, own, side_send.at[from_z, half], {"grp": 1 - g})

    def slot_arrived(slot, half):
        text_copy(slot, half, False, up_send.at[0, half], {"grp": 1 - g}).wait_recv()

    def sends_up(step):
        return (z >= step) & (z + 1 < tp_size)

    def sends_down(step):
        return (z + step < tp_size) & (z >= 1)

    def text_step(step, half):
        def forward():
            if step < tp_size - 1:

                @pl.when(sends_up(step))
                def _():
                    up_copy(step, half).start()

                @pl.when(sends_down(step))
                def _():
                    down_copy(step, half).start()

        if step == 0:
            forward()
            side_copy(z, half, True).start()
            return
        arriving = [(z - step, z >= step), (z + step, z + step < tp_size)]
        for from_z, there in arriving:

            @pl.when(there)
            def _():
                slot_arrived(from_z * grp_size + g, half)

        forward()
        for from_z, there in arriving:

            @pl.when(there)
            def _():
                side_copy(from_z, half, False).start()

    def nearest(k):
        found = jnp.int32(0)
        for at in range(tp_size):
            order = sorted(range(tp_size), key=lambda other: (abs(other - at), other))
            found = found + (z == at).astype(jnp.int32) * order[k]
        return found

    def gained(slot, at=pl.ds(0, tokens_dev)):
        columns = pl.ds(pl.multiple_of(slot * width, width), width)
        piece = full[slot, at].astype(F32)
        square = jnp.sum(piece * piece, axis=-1, keepdims=True)
        return (piece * ngain[:, columns]).astype(BF16), square, columns

    def project(piece, columns, weight):
        return jnp.dot(piece, weight[columns, :], preferred_element_type=F32)

    def side_slot(k):
        slot = nearest(k) * grp_size + 1 - g
        for half in range(HALVES):
            slot_arrived(slot, half)
        return slot

    def take(slot, squares):
        piece, square, columns = gained(slot)
        if squares is None:
            kv_sum[...] = project(piece, columns, wkv_v)
            q_sum[...] = project(piece, columns, wq_v)
            return square
        kv_sum[...] += project(piece, columns, wkv_v)
        q_sum[...] += project(piece, columns, wq_v)
        return squares + square

    rs_copies = []
    for i, (other, where) in enumerate(tensor_peers):
        copy = remote(
            rs_send.at[other], rs_recv.at[mine], rs_send_sem.at[i], rs_recv_sem.at[mine], where
        )
        copy.start()
        rs_copies.append(copy)
    for half in range(HALVES):
        text_step(0, half)
    late = -(-vis_rows // 16) * 16
    slot_of = lax.broadcasted_iota(jnp.int32, (late, vis_rows), 0)
    row_of = lax.broadcasted_iota(jnp.int32, (late, vis_rows), 1)
    chosen = jnp.zeros((late, vis_rows), F32)
    start = jnp.int32(0)
    for source in range(ctx_size):
        count = route[source, c]
        for j in range(bucket):
            at = jnp.where(j < count, start + j, -1)
            hit = (slot_of == at) & (row_of == source * bucket + j)
            chosen = jnp.where(hit, 1.0, chosen)
        start = start + count
    chosen = chosen.astype(BF16)
    is_visual = lax.broadcasted_iota(jnp.int32, (late, 1), 0) < start

    own_text.wait()
    kv_load.wait()
    q_load.wait()
    squares = take(mine, None)
    for half in range(HALVES):
        text_step(1, half)
    total = rs_send[mine].astype(F32)
    for i, (other, where) in enumerate(tensor_peers):
        remote(
            rs_send.at[other], rs_recv.at[other], rs_send_sem.at[i], rs_recv_sem.at[other], where
        ).wait_recv()
        total = total + rs_recv[other].astype(F32)
    total = total.astype(BF16).astype(merged.dtype)
    for d in range(ctx_size):
        merged[d] = total[d * bucket : (d + 1) * bucket, :]

    row_copies = []
    for i, (other, where) in enumerate(ctx_peers):
        copy = remote(
            merged.at[other], arrived.at[c], row_send.at[i], row_recv.at[c], where
        )
        copy.start()
        row_copies.append(copy)
    row_keep = pltpu.make_async_copy(merged.at[c], arrived.at[c], row_own)
    row_keep.start()
    squares = take(side_slot(0), squares)
    for step in range(2, tp_size - 1):
        text_step(step, 0)
        squares = take(nearest(step - 1) * grp_size + g, squares)
        for half in range(1, HALVES):
            text_step(step, half)
        squares = take(side_slot(step - 1), squares)
    row_keep.wait()
    for i, (other, where) in enumerate(ctx_peers):
        remote(
            merged.at[other], arrived.at[other], row_send.at[i], row_recv.at[other], where
        ).wait_recv()
    for source in range(ctx_size):
        vis_mine[source * bucket : (source + 1) * bucket, :] = arrived[source]
    vis_send_rows[...] = vis_mine[...].astype(BF16)
    vis_copies = []

    def vis_copy(slot, sem, own, where):
        src = vis_send_rows if own else gathered.at[slot]
        return remote(src, gathered.at[slot], vis_send.at[sem], vis_recv.at[slot], where)

    line_peers = [lax.rem(z + step, tp_size) for step in range(1, tp_size)]
    for i, other in enumerate(line_peers):
        vis_copies.append(vis_copy(mine, i, True, {"tp": other}))
    vis_copies.append(vis_copy(mine, tp_size - 1, True, {"grp": 1 - g}))
    for copy in vis_copies:
        copy.start()

    def share_visual():
        for i, other in enumerate(line_peers):
            slot = other * grp_size + g
            vis_copy(slot, i, False, {"tp": other}).wait_recv()
            copy = vis_copy(slot, tp_size + i, False, {"grp": 1 - g})
            copy.start()
            vis_copies.append(copy)

    gathered[mine] = vis_send_rows[...]
    squares = take(nearest(tp_size - 2) * grp_size + g, squares)
    squares = take(side_slot(tp_size - 2), squares)

    near_slot = nearest(tp_size - 1) * grp_size + g
    far_slot = nearest(tp_size - 1) * grp_size + 1 - g

    def kv_copy(i, where, block, half):
        if half == 0:
            span_rows = pl.ds(late, half_rows - late)
        elif half == HALVES:
            span_rows = pl.ds(0, late)
        else:
            span_rows = part_of(half)
        return remote(
            kv_full.at[block, span_rows],
            kv_full.at[block, span_rows],
            kv_send.at[i, half],
            kv_recv.at[block, half],
            where,
        )

    kv_copies = []
    for half in range(HALVES):
        text_step(tp_size - 1, half)
        at = part_of(half)
        near_piece, near_square, near_columns = gained(near_slot, at)
        kv_now = kv_sum[at, :] + project(near_piece, near_columns, wkv_v)
        slot_arrived(far_slot, half)
        far_piece, far_square, far_columns = gained(far_slot, at)
        square = squares[half * half_rows : (half + 1) * half_rows] + near_square + far_square
        scale = lax.rsqrt(square / (members * width) + EPSILON)
        kv_now = (kv_now + project(far_piece, far_columns, wkv_v)) * scale
        kv_full[c, at, :] = kv_now.astype(BF16)
        for i, (other, where) in enumerate(ctx_peers):
            copy = kv_copy(i, where, c, half)
            copy.start()
            kv_copies.append(copy)
        q_now = q_sum[at, :] + project(near_piece, near_columns, wq_v)
        q_now = (q_now + project(far_piece, far_columns, wq_v)) * scale
        queries[at, :] = q_now.astype(BF16)
        if half == 0:
            share_visual()

    mine_row = jnp.broadcast_to(seg[pl.ds(c, 1), :], (tokens_dev, tokens_dev))
    query_seg = mine_row.T
    lane = lax.broadcasted_iota(jnp.int32, (tokens_dev, tokens_dev), 1)
    row = lax.broadcasted_iota(jnp.int32, (tokens_dev, tokens_dev), 0)
    query_pos = c * tokens_dev + row
    allowed = []
    for block in range(ctx_size):
        count = route[0, block]
        for source in range(1, ctx_size):
            count = count + route[source, block]
        near = (lane < count) | (block * tokens_dev + lane <= query_pos)
        allowed.append((query_seg == seg[block : block + 1, :]) & near)
    bias = jnp.concatenate([jnp.where(ok, 0.0, NEGATIVE) for ok in allowed], axis=1)

    for other in range(tp_size):
        vis_copy(other * grp_size + 1 - g, 0, False, {"grp": 1 - g}).wait_recv()
    visual = jnp.concatenate([gathered[t].astype(F32) for t in range(members)], axis=1)
    scale = lax.rsqrt(jnp.mean(visual * visual, axis=-1, keepdims=True) + EPSILON)
    visual = (visual * scale * ngain[...]).astype(BF16)
    visual = jnp.dot(chosen, visual, preferred_element_type=F32).astype(BF16)
    kv_rows = jnp.dot(visual, wkv_v[...], preferred_element_type=F32)
    kv_full[c, 0:late, :] = jnp.where(
        is_visual, kv_rows, kv_full[c, 0:late, :].astype(F32)
    ).astype(BF16)
    for i, (other, where) in enumerate(ctx_peers):
        copy = kv_copy(i, where, c, HALVES)
        copy.start()
        kv_copies.append(copy)
    query_rows = jnp.dot(visual, wq_v[...], preferred_element_type=F32)
    queries[0:late, :] = jnp.where(
        is_visual, query_rows, queries[0:late, :].astype(F32)
    ).astype(BF16)

    for i, (other, where) in enumerate(ctx_peers):
        for half in range(HALVES + 1):
            kv_copy(i, where, other, half).wait_recv()
    keys = jnp.concatenate([kv_full[b, :, :HD] for b in range(ctx_size)], axis=0)
    values = jnp.concatenate([kv_full[b, :, HD:] for b in range(ctx_size)], axis=0)
    for h in range(heads_dev):
        query = queries[:, h * HD : (h + 1) * HD]
        scores = lax.dot_general(
            query, keys, (((1,), (1,)), ((), ())), preferred_element_type=F32
        )
        scores = jnp.where(bias == 0.0, scores * HD ** (-0.5), NEGATIVE)
        weights = jnp.exp(scores - jnp.max(scores, axis=-1, keepdims=True))
        total = jnp.sum(weights, axis=-1, keepdims=True)
        mixed = jnp.dot(weights.astype(BF16), values, preferred_element_type=F32)
        out[:, h * HD : (h + 1) * HD] = (mixed / total).astype(BF16)

    for half in range(HALVES):
        for step in range(tp_size - 1):

            @pl.when(sends_up(step))
            def _():
                up_copy(step, half).wait_send()

            @pl.when(sends_down(step))
            def _():
                down_copy(step, half).wait_send()

        for from_z in range(tp_size):
            side_copy(from_z, half, False).wait_send()
    for copy in rs_copies + row_copies + vis_copies + kv_copies:
        copy.wait_send()


def fused(
    patches,
    route_count,
    text_states,
    segment_ids,
    vision_gain,
    merge_up,
    merge_down,
    norm_gain,
    query_weight,
    kv_weight,
):
    ctx_size = lax.axis_size("ctx")
    tp_size = lax.axis_size("tp")
    grp_size = lax.axis_size("grp")
    members = tp_size * grp_size
    rows = patches.shape[0]
    bucket = rows // ctx_size
    tokens_dev, width = text_states.shape
    features = query_weight.shape[0]
    vmem = pl.BlockSpec(memory_space=pltpu.VMEM)
    anywhere = pl.BlockSpec(memory_space=pl.ANY)
    scalars = pl.BlockSpec(memory_space=pltpu.SMEM)
    dma = pltpu.SemaphoreType.DMA
    kernel = functools.partial(body, ctx_size, tp_size, grp_size, KVH // tp_size)
    return pl.pallas_call(
        kernel,
        out_shape=pltpu.VMEM((tokens_dev, query_weight.shape[1]), BF16),
        in_specs=[
            vmem,
            scalars,
            anywhere,
            vmem,
            vmem,
            anywhere,
            anywhere,
            vmem,
            anywhere,
            anywhere,
        ],
        out_specs=vmem,
        scratch_shapes=[
            pltpu.VMEM(merge_up.shape[::-1], BF16),
            pltpu.VMEM(merge_down.shape, BF16),
            pltpu.VMEM(query_weight.shape, BF16),
            pltpu.VMEM((features, 2 * HD), BF16),
            pltpu.VMEM((members, tokens_dev, width), BF16),
            pltpu.VMEM((members, rows, width), BF16),
            pltpu.VMEM((members, rows, width), BF16),
            pltpu.VMEM((ctx_size, bucket, width), F32),
            pltpu.VMEM((ctx_size, bucket, width), F32),
            pltpu.VMEM((members, rows, width), BF16),
            pltpu.VMEM((rows, width), F32),
            pltpu.VMEM((rows, width), BF16),
            pltpu.VMEM((tokens_dev, 2 * HD), F32),
            pltpu.VMEM((tokens_dev, query_weight.shape[1]), F32),
            pltpu.VMEM((tokens_dev, query_weight.shape[1]), BF16),
            pltpu.VMEM((ctx_size, tokens_dev, 2 * HD), BF16),
            dma((patches.shape[1] // vision_gain.shape[0] + 3,)),
            dma,
            dma((members, HALVES)),
            dma((tp_size, HALVES)),
            dma((tp_size, HALVES)),
            dma((tp_size, HALVES)),
            dma((members,)),
            dma((members,)),
            dma((ctx_size,)),
            dma((ctx_size,)),
            dma,
            dma((members,)),
            dma((members,)),
            dma((ctx_size, HALVES + 1)),
            dma((ctx_size, HALVES + 1)),
        ],
        compiler_params=pltpu.CompilerParams(
            collective_id=0, has_side_effects=True, vmem_limit_bytes=56 * 2**20
        ),
    )(
        patches,
        route_count,
        text_states,
        segment_ids.reshape(ctx_size, tokens_dev),
        vision_gain.reshape(-1, HD),
        merge_up.T,
        merge_down,
        norm_gain.reshape(1, -1),
        query_weight,
        kv_weight,
    )


def solution(mesh):
    return jax.shard_map(
        fused if fits(mesh) else shards_wide,
        mesh=mesh,
        in_specs=(
            P("ctx", None),
            P(),
            P("ctx", ("tp", "grp")),
            P(),
            P(),
            P(None, ("tp", "grp")),
            P(("tp", "grp"), None),
            P(),
            P(None, ("tp", "grp")),
            P(None, "tp"),
        ),
        out_specs=P("ctx", ("tp", "grp")),
        check_vma=False,
    )
```
